128 devices in a mesh: tp: 4 (over z_lo, core), ep: 32 (over y, x, z_hi).
Axes of the slice: x: 4, y: 4, z: 4 (z_hi: 2, z_lo: 2; z = z_hi * 2 + z_lo), core: 2. Of those that a mesh axis runs over, the one named last changes fastest.
Arguments:
- hidden_in: bfloat16 [4096, 7168], P('ep', 'tp'), may hold values from -6 to 6
- next_ids: int32 [4096], P('ep'), may hold values from 0 to 65535, as said below
- embed_table: bfloat16 [65536, 7168], P('ep', 'tp'), may hold values from -6 to 6
- hidden_gain: float32 [7168], replicated, may hold values from 0.5 to 1.5
- embed_gain: float32 [7168], replicated, may hold values from 0.5 to 1.5
- ffn_gain: float32 [7168], P('tp'), may hold values from 0.5 to 1.5
- proj_weight: bfloat16 [2, 7168, 7168], P(None, 'ep', 'tp'), may hold values from -0.046875 to 0.046875
- routes: int32 [4096, 8], P('ep'), may hold values from 0 to 31, all different within a row; in each aligned block of 128 rows (0 to 127, 128 to 255, ...) at most 40 rows name the same one
- route_weights: float32 [4096, 8], P('ep'), may hold values from 0.05 to 0.5
- w_gate_up: bfloat16 [32, 7168, 2, 1024], P('ep', 'tp'), may hold values from -0.0625 to 0.0625
- w_down: bfloat16 [32, 1024, 7168], P('ep', None, 'tp'), may hold values from -0.1875 to 0.1875
- shared_gate_up: bfloat16 [7168, 2, 1024], P(('tp', 'ep')), may hold values from -0.0625 to 0.0625
- shared_down: bfloat16 [1024, 7168], P('ep', 'tp'), may hold values from -0.1875 to 0.1875
Outputs:
- module_out: bfloat16 [4096, 7168], P('ep', 'tp')
The draws below stay inside these ranges and needn't reach their ends.
Inputs may be any that keep to these rules, and one draw needn't show every extreme that they name: `routes`: each row names 8 different experts. Among the 128 rows of one index of ep no expert is named by more than 40 rows, and in some of them one expert is named by exactly 40. `next_ids`: vocabulary row v lies with index v // 2048 of ep. Among the 128 tokens of one index of ep at most 8 have their next token with one such index, and in every index of ep one is reached by exactly 8.
All inputs are finite; a program needn't handle non-finite values.
Results may differ from the reference program's by a relative error of at most 0.03.
Values may be sent and summed in bfloat16 or wider, within the bound.
No kernel may reach another device: no remote copies, remote signals or barrier semaphores. Data moves between devices by JAX's collectives and lax.ppermute only.
A program may use at most 128 MiB of HBM per device.

```python
import math
import jax
import jax.numpy as jnp
import numpy as np
from jax import lax

D = 7168
EH = 1024
SH = 1024
TOP = 8
VOCAB_DEV = 2048
TOK_DEV = 128
TOKENS = 4096
EXPERTS = 32
VOCAB = 65536
CAP = 40
IDCAP = 8
N_EP = 32


def draw_next_ids(key, part):
    blocks = TOKENS // TOK_DEV
    holders_count = VOCAB // VOCAB_DEV

    def one_block(index):
        block_key = jax.random.fold_in(jax.random.fold_in(key, 7101), index)
        keys = jax.random.split(block_key, 5)
        busiest = jax.random.randint(keys[0], (), 0, holders_count).astype(jnp.int32)
        others = jax.random.permutation(keys[1], (holders_count - 1) * IDCAP)[:TOK_DEV - IDCAP] // IDCAP
        others = (others + (others >= busiest).astype(jnp.int32)).astype(jnp.int32)
        holders = jnp.concatenate([jnp.full((IDCAP,), busiest, jnp.int32), others])
        holders = holders[jax.random.permutation(keys[2], TOK_DEV)]
        reach = jax.random.randint(keys[3], (TOK_DEV,), 1, VOCAB_DEV + 1)
        local = jax.random.randint(keys[4], (TOK_DEV,), 0, reach)
        return (holders * VOCAB_DEV + local).astype(jnp.int32)
    return jax.vmap(one_block)(jnp.arange(blocks, dtype=jnp.int32)).reshape(-1)


def shard_levels(rng, shape, cuts, least, high):
    def one(dim, shards_of):
        steps = jax.random.uniform(jax.random.fold_in(jax.random.fold_in(rng, 6), dim), (shards_of,), jnp.float32, least / len(cuts), high / len(cuts))
        return jnp.repeat(jnp.exp(steps), shape[dim] // shards_of).reshape((-1,) + (1,) * (len(shape) - dim - 1))

    loudness = one(*cuts[0])
    for cut in cuts[1:]:
        loudness = loudness * one(*cut)
    return loudness


def assign_block(stream_key, own, number, rows, amount, top, most, lean):
    ranking = jax.random.permutation(stream_key, amount)
    heavy_load, usual = shares(amount, rows * top, most, lean, True), shares(amount, rows * top, most, lean, False)
    places = jnp.arange(amount)

    def named(lengths, turn):
        used = int((lengths > 0).sum())
        fixed = max(1, used // 4)
        passed = fixed + (places - fixed + turn * (used - fixed)) % max(1, amount - fixed)
        return jnp.zeros((amount,), jnp.int32).at[ranking[jnp.where(places < fixed, places, passed)]].set(jnp.asarray(lengths, jnp.int32))

    lengths = jnp.where(number % 4 == 0, named(heavy_load, number // 4), named(usual, number - number // 4 - 1))
    mixed = jax.random.permutation(jax.random.fold_in(own, 3), amount)
    source_of, receiver = mixed[0:amount // 2 * 2:2], mixed[1:amount // 2 * 2:2]
    room = jnp.minimum(lengths[source_of] - 1, most - lengths[receiver]) // 2
    room = jnp.where((source_of == ranking[0]) | (receiver == ranking[0]) | (lengths[receiver] == 0), 0, jnp.maximum(room, 0))
    passed = jax.random.randint(jax.random.fold_in(own, 4), (amount // 2,), 0, 1 << 20) % (room + 1)
    lengths = lengths.at[source_of].add(-passed).at[receiver].add(passed)
    labels = jnp.searchsorted(jnp.cumsum(lengths), jnp.arange(rows * top), side="right").astype(jnp.int32)
    listing = labels.reshape(top, rows).T
    listing = listing[jax.random.permutation(jax.random.fold_in(own, 1), rows)]
    turn = jax.random.randint(jax.random.fold_in(own, 2), (rows, 1), 0, top)
    return jnp.take_along_axis(listing, (jnp.arange(top)[None, :] + turn) % top, axis=1)


def shares(number_of, total, most, skew, full):
    portions = [(1 << 20) // math.isqrt(rank ** skew) + 1 for rank in range(1, number_of + 1)]
    largest = most if full else min(most, max(-(-total // number_of), total * portions[0] // sum(portions)))
    least = 1 if total - largest >= number_of - 1 else 0
    holding, spare = [largest] + [least] * (number_of - 1), total - largest - least * (number_of - 1)
    while spare > 0:
        candidates = [i for i in range(1, number_of) if holding[i] < largest] or [i for i in range(1, number_of) if holding[i] < most]
        mass, remaining = sum([portions[i] for i in candidates]), spare
        for i in candidates:
            addition = min(most - holding[i], max(1, remaining * portions[i] // mass), spare)
            holding[i] = holding[i] + addition
            spare = spare - addition
    return np.array(holding)


def gaussian(rng, extent, scale, most, cuts=(), held_as=jnp.bfloat16):
    drawn = jax.random.normal(rng, extent, jnp.float32) * scale
    if len(cuts) > 0:
        drawn = shard_levels(rng, extent, cuts, -0.22, 0.18) * drawn
    return jnp.clip(drawn, min=-most, max=most).astype(held_as)


def setup_inputs(seed: int = 0) -> dict:
    seeds = jax.random.split(jax.random.key(seed), 14)
    hidden_in = gaussian(seeds[0], (TOKENS, D), 1.0, 6.0, ((0, 32), (1, 4)))
    next_ids = draw_next_ids(jax.random.fold_in(seeds[13], 71), 0)
    embed_table = gaussian(seeds[2], (VOCAB, D), 1.0, 6.0, ((0, 32), (1, 4)))
    hidden_gain = jnp.clip(1.0 + 0.1 * jax.random.normal(seeds[3], (D,), jnp.float32), 0.5, 1.5)
    embed_gain = jnp.clip(1.0 + 0.1 * jax.random.normal(seeds[4], (D,), jnp.float32), 0.5, 1.5)
    ffn_gain = jnp.clip(1.0 + 0.1 * jax.random.normal(seeds[5], (D,), jnp.float32), 0.5, 1.5)
    proj_weight = gaussian(seeds[6], (2, D, D), (2 * D) ** -0.5, 0.046875, ((1, 32), (2, 4)))
    routes_keys = jax.random.split(jax.random.fold_in(seeds[7], 1), TOKENS // TOK_DEV)
    routes_turns = jax.random.permutation(jax.random.fold_in(seeds[7], 3), TOKENS // TOK_DEV)
    routes = jax.vmap(lambda own, number: assign_block(jax.random.fold_in(seeds[7], 2), own, number, TOK_DEV, EXPERTS, TOP, CAP, 2))(routes_keys, routes_turns).reshape((TOKENS, TOP))
    route_weights = jnp.clip(jnp.exp(math.log(0.5) - 2.3025851 * jax.random.uniform(seeds[8], (TOKENS, TOP), jnp.float32) ** shard_levels(seeds[8], (TOKENS, TOP), ((0, 32),), -0.2, 0.2)), 0.05, 0.5)
    w_gate_up = gaussian(seeds[9], (EXPERTS, D, 2, EH), D ** -0.5, 0.0625, ((0, 32), (1, 4)))
    w_down = gaussian(seeds[10], (EXPERTS, EH, D), EH ** -0.5, 0.1875, ((0, 32), (2, 4)))
    shared_gate_up = gaussian(seeds[11], (D, 2, SH), D ** -0.5, 0.0625, ((0, 128),))
    shared_down = gaussian(seeds[12], (SH, D), SH ** -0.5, 0.1875, ((0, 32), (1, 4)))
    return dict(hidden_in=hidden_in, next_ids=next_ids, embed_table=embed_table, hidden_gain=hidden_gain, embed_gain=embed_gain, ffn_gain=ffn_gain, proj_weight=proj_weight, routes=routes, route_weights=route_weights, w_gate_up=w_gate_up, w_down=w_down, shared_gate_up=shared_gate_up, shared_down=shared_down)


def rms_norm(values, gain):
    values = values.astype(jnp.float32)
    scale = lax.rsqrt(lax.optimization_barrier(jnp.mean(values * values, axis=-1, keepdims=True)) + 1e-06)
    return (values * scale * gain).astype(jnp.bfloat16)

def gated(pair):
    return (jax.nn.silu(pair[:, 0]) * pair[:, 1]).astype(jnp.bfloat16)

def reference(hidden_in, next_ids, embed_table, hidden_gain, embed_gain, ffn_gain, proj_weight, routes, route_weights, w_gate_up, w_down, shared_gate_up, shared_down):
    embedded = embed_table[next_ids]
    hidden_normed = rms_norm(hidden_in, hidden_gain)
    embed_normed = rms_norm(embedded, embed_gain)
    joined = jnp.stack([hidden_normed, embed_normed], axis=1)
    block_width = D // N_EP
    blocks = joined.reshape(TOKENS, 2, N_EP, block_width).transpose(2, 0, 1, 3).reshape(N_EP, TOKENS, 2 * block_width)
    weights = proj_weight.reshape(2, N_EP, block_width, D).transpose(1, 0, 2, 3).reshape(N_EP, 2 * block_width, D)

    def add_block(total, both):
        part = jnp.dot(both[0], both[1], preferred_element_type=jnp.float32).astype(jnp.bfloat16)
        part = lax.optimization_barrier(part)
        return (total + part.astype(jnp.float32), None)
    summed, _ = lax.scan(add_block, jnp.zeros((TOKENS, D), jnp.float32), (blocks, weights))
    projected = summed.astype(jnp.bfloat16)
    normed = rms_norm(projected, ffn_gain)
    limit = N_EP * CAP
    token_index = jnp.arange(TOKENS, dtype=jnp.int32)
    gate_up_flat = w_gate_up.reshape(EXPERTS, D, 2 * EH)

    def one_expert(expert, routed):
        marked = routes == expert
        chosen = jnp.any(marked, axis=1)
        weight = lax.optimization_barrier(jnp.sum(jnp.where(marked, route_weights, 0.0), axis=1))
        place = (jnp.cumsum(chosen.astype(jnp.int32)) - 1).astype(jnp.int32)
        target = jnp.where(chosen, place, limit).astype(jnp.int32)
        index = jnp.zeros((limit,), jnp.int32).at[target].set(token_index, mode='drop')
        valid = jnp.arange(limit, dtype=jnp.int32) < jnp.sum(chosen.astype(jnp.int32))
        rows = normed[index]
        pair = jnp.dot(rows, gate_up_flat[expert], preferred_element_type=jnp.float32).reshape(limit, 2, EH)
        act = gated(pair)
        expert_out = jnp.dot(act, w_down[expert], preferred_element_type=jnp.float32).astype(jnp.bfloat16)
        term = jnp.where(valid[:, None], weight[index][:, None] * expert_out.astype(jnp.float32), 0.0)
        return routed.at[index].add(term)
    routed = lax.fori_loop(0, EXPERTS, one_expert, jnp.zeros((TOKENS, D), jnp.float32))
    shared_pair = jnp.dot(normed, shared_gate_up.reshape(D, 2 * SH), preferred_element_type=jnp.float32).reshape(TOKENS, 2, SH)
    shared_act = gated(shared_pair)
    shared = jnp.dot(shared_act, shared_down, preferred_element_type=jnp.float32)
    return (projected.astype(jnp.float32) + routed + shared).astype(jnp.bfloat16)
```

```python
import jax
import jax.numpy as jnp
from jax import lax
from jax.experimental import pallas as pl
from jax.experimental.pallas import tpu as pltpu
from jax.sharding import Mesh
from jax.sharding import PartitionSpec as P

EP = ("ep_0", "ep_1", "ep_2")
XZ = ("ep_1", "ep_2")
TP_EP = ("tp", "ep_0", "ep_1", "ep_2")
BF = jnp.bfloat16
F32 = jnp.float32


def params(*semantics):
    return pltpu.CompilerParams(dimension_semantics=semantics)


def cost(flops, moved):
    return pl.CostEstimate(flops=int(flops), bytes_accessed=int(moved), transcendentals=0)


def swap(value, bit):
    return lax.ppermute(value, "tp", [(i, i ^ bit) for i in range(4)])


def copies(value, axes, count):
    spread = jnp.broadcast_to(value[None], (count, *value.shape))
    return lax.all_to_all(spread, axes, split_axis=0, concat_axis=0, tiled=True)


def feature_blocks(rows, scale, gain, count):
    n, width = rows.shape
    part = width // count

    def kernel(x_ref, s_ref, g_ref, o_ref):
        v = x_ref[...].astype(F32) * s_ref[...] * g_ref[...]
        for b in range(count):
            o_ref[b] = v[:, b * part : (b + 1) * part].astype(BF)

    return pl.pallas_call(
        kernel,
        out_shape=jax.ShapeDtypeStruct((count, n, part), BF),
        cost_estimate=cost(4 * n * width, 4 * n * width),
    )(rows, scale, gain)


def found_blocks(ids, table, scales, gain, planes, count):
    slots = ids.shape[0]
    vocab, width = table.shape
    part = width // count
    step = 512
    each = slots // planes

    def kernel(i_ref, t_ref, s_ref, g_ref, o_ref, acc, sc):
        k = pl.program_id(0)

        @pl.when(k == 0)
        def _():
            acc[...] = jnp.zeros_like(acc)
            sc[...] = jnp.zeros_like(sc)

        hit = i_ref[:, 0:1] - 1 == lax.broadcasted_iota(jnp.int32, (slots, step), 1) + k * step
        acc[...] += jnp.dot(
            jnp.where(hit, 1.0, 0.0).astype(BF), t_ref[...], preferred_element_type=F32
        )
        sc[...] += jnp.sum(jnp.where(hit, s_ref[...], 0.0), axis=1, keepdims=True)

        @pl.when(k == pl.num_programs(0) - 1)
        def _():
            v = acc[...] * sc[...] * g_ref[...]
            for b in range(count):
                piece = v[:, b * part : (b + 1) * part].astype(BF)
                for y in range(planes):
                    o_ref[y, b] = piece[y * each : (y + 1) * each]

    return pl.pallas_call(
        kernel,
        grid=(vocab // step,),
        in_specs=[
            pl.BlockSpec((slots, ids.shape[1]), lambda k: (0, 0)),
            pl.BlockSpec((step, width), lambda k: (k, 0)),
            pl.BlockSpec((1, step), lambda k: (0, k)),
            pl.BlockSpec((1, width), lambda k: (0, 0)),
        ],
        out_specs=pl.BlockSpec((planes, count, each, part), lambda k: (0, 0, 0, 0)),
        out_shape=jax.ShapeDtypeStruct((planes, count, each, part), BF),
        scratch_shapes=[pltpu.VMEM((slots, width), F32), pltpu.VMEM((slots, 1), F32)],
        compiler_params=params("arbitrary"),
        cost_estimate=cost(2 * slots * vocab * width, 2 * vocab * width),
    )(ids, table, scales, gain)


def picked_blocks(arrived, places, tokens):
    holders, rows, part = arrived.shape
    sources = places.shape[0]
    each = rows // sources
    slots = holders * each

    def kernel(a_ref, p_ref, o_ref):
        hit = lax.broadcasted_iota(jnp.int32, (slots, tokens), 0) == p_ref[0, 0:1, :]
        o_ref[0] = lax.dot_general(
            jnp.where(hit, 1.0, 0.0).astype(BF),
            a_ref[...].reshape(slots, part),
            (((0,), (0,)), ((), ())),
            preferred_element_type=F32,
        ).astype(BF)

    return pl.pallas_call(
        kernel,
        grid=(sources,),
        in_specs=[
            pl.BlockSpec((holders, each, part), lambda s: (0, s, 0)),
            pl.BlockSpec((1, places.shape[1], tokens), lambda s: (s, 0, 0)),
        ],
        out_specs=pl.BlockSpec((1, tokens, part), lambda s: (s, 0, 0)),
        out_shape=jax.ShapeDtypeStruct((sources, tokens, part), BF),
        compiler_params=params("arbitrary"),
        cost_estimate=cost(2 * sources * slots * tokens * part, 4 * holders * rows * part),
    )(arrived, places)


def partial_projection(index, acts, weights, half, start, out_type):
    rows, part = acts[0].shape
    width = weights.shape[3]
    tile = 256

    def kernel(idx, *refs):
        a, w, rest = refs[:4], refs[4:8], refs[8:]
        total = rest[0][...] if start is not None else None
        for q in range(4):
            term = jnp.dot(a[q][...], w[q][0, 0], preferred_element_type=F32)
            total = term if total is None else total + term
        rest[-1][...] = total.astype(out_type)

    def weight_spec(q):
        return pl.BlockSpec((1, 1, part, tile), lambda n, idx: (idx[q], half, 0, n))

    in_specs = [pl.BlockSpec((rows, part), lambda n, idx: (0, 0))] * 4
    in_specs += [weight_spec(q) for q in range(4)]
    operands = [*acts, *([weights] * 4)]
    if start is not None:
        in_specs.append(pl.BlockSpec((rows, tile), lambda n, idx: (0, n)))
        operands.append(start)
    return pl.pallas_call(
        kernel,
        grid_spec=pltpu.PrefetchScalarGridSpec(
            num_scalar_prefetch=1,
            grid=(width // tile,),
            in_specs=in_specs,
            out_specs=pl.BlockSpec((rows, tile), lambda n, idx: (0, n)),
        ),
        out_shape=jax.ShapeDtypeStruct((rows, width), out_type),
        compiler_params=params("arbitrary"),
        cost_estimate=cost(8 * rows * part * width, 6 * rows * width),
    )(index, *operands)


def gained_columns(weights, gain, count):
    depth, _, width = weights.shape
    part = width // count
    step = 256

    def kernel(w_ref, g_ref, o_ref):
        g = g_ref[...]
        o_ref[0, :, 0:part] = (w_ref[:, 0, :].astype(F32) * g).astype(BF)
        o_ref[0, :, part : 2 * part] = (w_ref[:, 1, :].astype(F32) * g).astype(BF)

    return pl.pallas_call(
        kernel,
        grid=(depth // step, count),
        in_specs=[
            pl.BlockSpec((step, 2, part), lambda k, t: (k, 0, t)),
            pl.BlockSpec((step, 1), lambda k, t: (k, 0)),
        ],
        out_specs=pl.BlockSpec((1, step, 2 * part), lambda k, t: (t, k, 0)),
        out_shape=jax.ShapeDtypeStruct((count, depth, 2 * part), BF),
        compiler_params=params("arbitrary", "arbitrary"),
        cost_estimate=cost(2 * depth * width, 8 * depth * width),
    )(weights, gain)


def column_products(index, rows, weights, count):
    n, depth = rows.shape
    part = weights.shape[2]

    def kernel(idx, x_ref, w_ref, o_ref):
        o_ref[0] = jnp.dot(x_ref[...], w_ref[0], preferred_element_type=F32).astype(BF)

    return pl.pallas_call(
        kernel,
        grid_spec=pltpu.PrefetchScalarGridSpec(
            num_scalar_prefetch=1,
            grid=(count,),
            in_specs=[
                pl.BlockSpec((n, depth), lambda b, idx: (0, 0)),
                pl.BlockSpec((1, depth, part), lambda b, idx: (idx[b], 0, 0)),
            ],
            out_specs=pl.BlockSpec((1, n, part), lambda b, idx: (b, 0, 0)),
        ),
        out_shape=jax.ShapeDtypeStruct((count, n, part), BF),
        compiler_params=params("arbitrary"),
        cost_estimate=cost(2 * count * n * depth * part, 2 * n * depth + 2 * count * depth * part),
    )(index, rows, weights)


def down_products(index, acts, weights):
    n, part = acts[0].shape
    width = weights.shape[1]
    tile = 256

    def kernel(idx, *refs):
        a, w, o_ref = refs[:4], refs[4:8], refs[8]
        total = None
        for q in range(4):
            term = jnp.dot(a[q][...], w[q][...], preferred_element_type=F32)
            total = term if total is None else total + term
        o_ref[...] = total.astype(BF)

    def weight_spec(q):
        return pl.BlockSpec((part, tile), lambda j, idx: (idx[q], j))

    return pl.pallas_call(
        kernel,
        grid_spec=pltpu.PrefetchScalarGridSpec(
            num_scalar_prefetch=1,
            grid=(width // tile,),
            in_specs=[pl.BlockSpec((n, part), lambda j, idx: (0, 0))] * 4
            + [weight_spec(q) for q in range(4)],
            out_specs=pl.BlockSpec((n, tile), lambda j, idx: (0, j)),
        ),
        out_shape=jax.ShapeDtypeStruct((n, width), BF),
        compiler_params=params("arbitrary"),
        cost_estimate=cost(8 * n * part * width, 2 * n * width),
    )(index, *acts, *([weights] * 4))


def ranked(marks):
    rows = marks.shape[0]
    below = jnp.tril(jnp.ones((rows, rows), BF), -1)
    return jnp.dot(below, marks.astype(BF), preferred_element_type=F32).astype(jnp.int32)


def on_device(
    hidden_in,
    next_ids,
    embed_table,
    hidden_gain,
    embed_gain,
    ffn_gain,
    proj_weight,
    routes,
    route_weights,
    w_gate_up,
    w_down,
    shared_gate_up,
    shared_down,
):
    tokens, width = hidden_in.shape
    ep = lax.axis_size(EP)
    plane = lax.axis_size(XZ)
    planes = ep // plane
    vocab = embed_table.shape[0]
    model = width * 4
    t = lax.axis_index("tp")
    order_q = jnp.stack([t, t ^ 1, t ^ 2, t ^ 3]).astype(jnp.int32)
    experts = jnp.arange(ep, dtype=jnp.int32)

    id_slots = 2 * tokens // ep
    holder = next_ids // vocab
    marks = holder[:, None] == experts[None, :]
    order = jnp.sum(jnp.where(marks, ranked(marks), 0), axis=1)
    place = holder * id_slots + order
    slot_list = jnp.arange(ep * id_slots, dtype=jnp.int32)
    local_id = next_ids - holder * vocab + 1
    asked = jnp.sum(jnp.where(slot_list[:, None] == place[None, :], local_id[None, :], 0), axis=1)
    asked = jnp.broadcast_to(asked.reshape(ep, id_slots, 1), (ep, id_slots, 128))
    ids = lax.all_to_all(asked, EP, split_axis=0, concat_axis=0, tiled=True)
    places = copies(jnp.broadcast_to(place[None, :], (8, tokens)), XZ, plane)

    wide_hidden = hidden_in.astype(F32)
    wide_table = embed_table.astype(F32)
    squares = jnp.concatenate(
        [jnp.sum(wide_table * wide_table, axis=1), jnp.sum(wide_hidden * wide_hidden, axis=1)]
    )
    squares = copies(squares.reshape(-1, 128), "tp", 4).sum(axis=0).reshape(-1)
    scales = lax.rsqrt(squares / model + 1e-06)
    hidden_gain = lax.dynamic_slice(hidden_gain, (t * width,), (width,))[None, :]
    embed_gain = lax.dynamic_slice(embed_gain, (t * width,), (width,))[None, :]

    weights = lax.all_gather(proj_weight, "ep_0", axis=0)
    piece = lax.all_gather(shared_gate_up, EP, axis=0, tiled=True)
    down = lax.all_gather(shared_down, EP, axis=0, tiled=True)

    def over_tp(blocks):
        own = blocks.reshape(plane * tokens, -1)
        other = swap(own, 2)
        return [own, swap(own, 1), other, swap(other, 1)]

    hidden_blocks = feature_blocks(hidden_in, scales[vocab:, None], hidden_gain, plane)
    hidden_blocks = lax.all_to_all(hidden_blocks, XZ, split_axis=0, concat_axis=0, tiled=True)
    start = partial_projection(order_q, over_tp(hidden_blocks), weights, 0, None, F32)

    found = found_blocks(
        ids.reshape(ep * id_slots, 128), embed_table, scales[None, :vocab], embed_gain, planes, plane
    )
    found = found.reshape(ep, plane * id_slots, -1)
    found = lax.all_to_all(found, EP, split_axis=0, concat_axis=0, tiled=True)
    embed_blocks = picked_blocks(found, places, tokens)
    partial = partial_projection(order_q, over_tp(embed_blocks), weights, 1, start, BF)

    top = routes.shape[1]
    capacity = min(tokens, tokens * top * 5 // (4 * ep))
    named = routes[:, :, None] == experts[None, None, :]
    hits = jnp.any(named, axis=1)
    share = jnp.sum(jnp.where(named, route_weights[:, :, None], 0.0), axis=1)
    rank = jnp.where(hits, ranked(hits), -1)
    taken = rank.T[:, None, :] == jnp.arange(capacity, dtype=jnp.int32)[None, :, None]
    send = taken.astype(BF).reshape(ep * capacity, tokens)
    combine = jnp.where(taken, share.T[:, None, :], 0.0).astype(BF)
    combine = combine.reshape(ep * capacity, tokens)

    partial = lax.all_to_all(
        partial.reshape(plane, tokens, width), XZ, split_axis=0, concat_axis=0, tiled=True
    )
    projected = partial.astype(F32).sum(axis=0).astype(BF)

    outgoing = jnp.dot(send, projected, preferred_element_type=F32).astype(BF)
    arrived = lax.all_to_all(
        outgoing.reshape(ep, capacity, width), EP, split_axis=0, concat_axis=0, tiled=True
    )

    wide = projected.astype(F32)
    squares = copies(jnp.sum(wide * wide, axis=1).reshape(1, tokens), "tp", 4).sum(axis=(0, 1))
    row_scale = lax.rsqrt(squares / model + 1e-06)
    sent_scale = jnp.sum(jnp.where(taken, row_scale[None, None, :], 0.0), axis=2)
    sent_scale = jnp.pad(sent_scale, ((0, 0), (0, 128 - capacity)))[:, None, :]
    slot_scale = lax.all_to_all(sent_scale, EP, split_axis=0, concat_axis=0, tiled=True)
    slot_scale = slot_scale[:, 0, :capacity].reshape(-1, 1)

    def gated(pair, scale):
        hidden = pair.shape[-1] // 2
        pair = pair * scale
        return (jax.nn.silu(pair[:, :hidden]) * pair[:, hidden:]).astype(BF)

    gain_column = ffn_gain[:, None]
    rows = arrived.reshape(ep * capacity, width)
    columns = gained_columns(w_gate_up, gain_column, 4)
    far = column_products(jnp.stack([t ^ 3, t ^ 1]).astype(jnp.int32), rows, columns, 2)
    far = swap(far, 1)
    near = column_products(jnp.stack([t ^ 2, t]).astype(jnp.int32), rows, columns, 2)
    across = swap((far[0].astype(F32) + near[0].astype(F32)).astype(BF), 2)
    pair = far[1].astype(F32) + near[1].astype(F32) + across.astype(F32)
    act = gated(pair, slot_scale)
    other = swap(act, 2)
    acts = [act, swap(act, 1), other, swap(other, 1)]
    down_block = w_down.reshape(w_down.shape[1], w_down.shape[2])
    result = down_products(order_q, acts, down_block)
    returned = lax.all_to_all(
        result.reshape(ep, capacity, width), EP, split_axis=0, concat_axis=0, tiled=True
    )

    shared_columns = gained_columns(piece, gain_column, 4)
    shared_pair = column_products(jnp.arange(4, dtype=jnp.int32), projected, shared_columns, 4)
    shared_pair = lax.all_to_all(shared_pair, "tp", split_axis=0, concat_axis=0, tiled=True)
    shared_act = gated(shared_pair.astype(F32).sum(axis=0), row_scale[:, None])
    shared_act = copies(shared_act, "tp", 4)
    shared_act = shared_act.transpose(1, 0, 2).reshape(tokens, -1)
    shared = jnp.dot(shared_act, down, preferred_element_type=F32)

    routed = lax.dot_general(
        combine,
        returned.reshape(ep * capacity, width),
        (((0,), (0,)), ((), ())),
        preferred_element_type=F32,
    )
    return (projected.astype(F32) + routed + shared).astype(BF)


def solution(mesh):
    finer = Mesh(mesh.devices.reshape(mesh.shape["tp"], 4, 4, 2), ("tp", "ep_0", "ep_1", "ep_2"))
    in_specs = (
        P(EP, "tp"),
        P(EP),
        P(EP, "tp"),
        P(),
        P(),
        P("tp"),
        P(None, EP, "tp"),
        P(EP, None),
        P(EP, None),
        P(EP, "tp", None, None),
        P(EP, None, "tp"),
        P(TP_EP, None, None),
        P(EP, "tp"),
    )
    out_specs = P(EP, "tp")

    def body(*args):
        args = list(args)
        args[9] = args[9].reshape(args[9].shape[1:])
        return on_device(*args)

    return jax.shard_map(body, mesh=finer, in_specs=in_specs, out_specs=out_specs, check_vma=False)
```

```python
import jax
import jax.numpy as jnp
from jax import lax
from jax.experimental import pallas as pl
from jax.experimental.pallas import tpu as pltpu
from jax.sharding import Mesh
from jax.sharding import PartitionSpec as P

EP = ("ep_0", "ep_1", "ep_2")
XZ = ("ep_1", "ep_2")
TP_EP = ("tp", "ep_0", "ep_1", "ep_2")
BF = jnp.bfloat16
F32 = jnp.float32


def params(*semantics):
    return pltpu.CompilerParams(dimension_semantics=semantics)


def cost(flops, moved):
    return pl.CostEstimate(flops=int(flops), bytes_accessed=int(moved), transcendentals=0)


def swap(value, bit):
    return lax.ppermute(value, "tp", [(i, i ^ bit) for i in range(4)])


def shift(value, axis, by):
    size = lax.axis_size(axis)
    return lax.ppermute(value, axis, [(i, (i + by) % size) for i in range(size)])


def after(value, *earlier):
    return lax.optimization_barrier((value, *earlier))[0]


def together(*values):
    return lax.optimization_barrier(values)


def stacked(value, axis, moved):
    me = lax.axis_index(axis)
    whole = jnp.zeros((4, *value.shape), value.dtype)
    for by, piece in moved.items():
        whole = lax.dynamic_update_index_in_dim(whole, piece, (me - by) % 4, 0)
    return lax.dynamic_update_index_in_dim(whole, value, me, 0)


def padded(part):
    return -(-part // 128) * 128


def feature_blocks(rows, scale, gain, count):
    n, width = rows.shape
    part = width // count
    room = padded(part)

    def kernel(x_ref, s_ref, g_ref, o_ref):
        v = x_ref[...].astype(F32) * s_ref[...] * g_ref[...]
        o_ref[...] = jnp.zeros_like(o_ref)
        for b in range(count):
            o_ref[b, :, 0:part] = v[:, b * part : (b + 1) * part].astype(BF)

    return pl.pallas_call(
        kernel,
        out_shape=jax.ShapeDtypeStruct((count, n, room), BF),
        cost_estimate=cost(4 * n * width, 4 * n * width),
    )(rows, scale, gain)


def found_blocks(asked, table, scales, gain, planes, count):
    holders, half = asked.shape[0], asked.shape[1] // 2
    slots = holders * half
    vocab, width = table.shape
    part = width // count
    room = padded(part)
    step = 512
    each = slots // planes

    def kernel(i_ref, t_ref, s_ref, g_ref, o_ref, acc, sc):
        k = pl.program_id(0)

        @pl.when(k == 0)
        def _():
            acc[...] = jnp.zeros_like(acc)
            sc[...] = jnp.zeros_like(sc)

        ids = i_ref[...].reshape(slots, 128)[:, 0:1] - 1
        hit = ids == lax.broadcasted_iota(jnp.int32, (slots, step), 1) + k * step
        acc[...] += jnp.dot(
            jnp.where(hit, 1.0, 0.0).astype(BF), t_ref[...], preferred_element_type=F32
        )
        sc[...] += jnp.sum(jnp.where(hit, s_ref[...], 0.0), axis=1, keepdims=True)

        @pl.when(k == pl.num_programs(0) - 1)
        def _():
            v = acc[...] * sc[...] * g_ref[...]
            o_ref[...] = jnp.zeros_like(o_ref)
            for b in range(count):
                piece = v[:, b * part : (b + 1) * part].astype(BF)
                for y in range(planes):
                    o_ref[y, b, :, 0:part] = piece[y * each : (y + 1) * each]

    return pl.pallas_call(
        kernel,
        grid=(vocab // step,),
        in_specs=[
            pl.BlockSpec((holders, half, 128), lambda k: (0, 0, 0)),
            pl.BlockSpec((step, width), lambda k: (k, 0)),
            pl.BlockSpec((1, step), lambda k: (0, k)),
            pl.BlockSpec((1, width), lambda k: (0, 0)),
        ],
        out_specs=pl.BlockSpec((planes, count, each, room), lambda k: (0, 0, 0, 0)),
        out_shape=jax.ShapeDtypeStruct((planes, count, each, room), BF),
        scratch_shapes=[pltpu.VMEM((slots, width), F32), pltpu.VMEM((slots, 1), F32)],
        compiler_params=params("arbitrary"),
        cost_estimate=cost(2 * slots * vocab * width, 2 * vocab * width),
    )(asked, table, scales, gain)


def picked_blocks(first, arrived, asked, sources, tokens):
    holders, rows, room = arrived.shape
    each = rows // sources
    slots = holders * each

    def kernel(f_ref, a_ref, p_ref, o_ref):
        hit = lax.broadcasted_iota(jnp.int32, (slots, tokens), 0) == p_ref[0, 0:1, :]
        o_ref[0] = lax.dot_general(
            jnp.where(hit, 1.0, 0.0).astype(BF),
            a_ref[...].reshape(slots, room),
            (((0,), (0,)), ((), ())),
            preferred_element_type=F32,
        ).astype(BF)

    return pl.pallas_call(
        kernel,
        grid_spec=pltpu.PrefetchScalarGridSpec(
            num_scalar_prefetch=1,
            grid=(sources,),
            in_specs=[
                pl.BlockSpec((holders, each, room), lambda s, f: (0, s, 0)),
                pl.BlockSpec((1, asked.shape[1] // 2, tokens), lambda s, f: (f[0] + s, 1, 0)),
            ],
            out_specs=pl.BlockSpec((1, tokens, room), lambda s, f: (s, 0, 0)),
        ),
        out_shape=jax.ShapeDtypeStruct((sources, tokens, room), BF),
        compiler_params=params("arbitrary"),
        cost_estimate=cost(2 * sources * slots * tokens * room, 4 * holders * rows * room),
    )(first, arrived, asked)


def gained_columns(blocks, weights, gain, count):
    depth, _, width = weights.shape
    part = width // count
    step = depth // 8
    picked = blocks.shape[0]

    def kernel(at, w_ref, g_ref, o_ref):
        g = g_ref[...]
        o_ref[:, 0:part] = (w_ref[:, 0, :].astype(F32) * g).astype(BF)
        o_ref[:, part : 2 * part] = (w_ref[:, 1, :].astype(F32) * g).astype(BF)

    return pl.pallas_call(
        kernel,
        grid_spec=pltpu.PrefetchScalarGridSpec(
            num_scalar_prefetch=1,
            grid=(8, picked),
            in_specs=[
                pl.BlockSpec((step, 2, part), lambda k, b, at: (k, 0, at[b])),
                pl.BlockSpec((step, 1), lambda k, b, at: (k, 0)),
            ],
            out_specs=pl.BlockSpec((step, 2 * part), lambda k, b, at: (k, b)),
        ),
        out_shape=jax.ShapeDtypeStruct((depth, picked * 2 * part), BF),
        compiler_params=params("arbitrary", "arbitrary"),
        cost_estimate=cost(2 * depth * width, 4 * depth * width),
    )(blocks, weights, gain)


def product(rows, weights):
    return jnp.dot(rows, weights, preferred_element_type=F32)


def ranked(marks):
    rows = marks.shape[0]
    below = jnp.tril(jnp.ones((rows, rows), BF), -1)
    return jnp.dot(below, marks.astype(BF), preferred_element_type=F32).astype(jnp.int32)


def on_device(
    hidden_in,
    next_ids,
    embed_table,
    hidden_gain,
    embed_gain,
    ffn_gain,
    proj_weight,
    routes,
    route_weights,
    w_gate_up,
    w_down,
    shared_gate_up,
    shared_down,
):
    tokens, width = hidden_in.shape
    ep = lax.axis_size(EP)
    plane = lax.axis_size(XZ)
    planes = ep // plane
    vocab = embed_table.shape[0]
    model = width * 4
    t = lax.axis_index("tp")
    y = lax.axis_index("ep_0")
    x = lax.axis_index("ep_1")
    z = lax.axis_index("ep_2")
    experts = jnp.arange(ep, dtype=jnp.int32)

    id_slots = 2 * tokens // ep
    holder = next_ids // vocab
    marks = holder[:, None] == experts[None, :]
    order = jnp.sum(jnp.where(marks, ranked(marks), 0), axis=1)
    place = holder * id_slots + order
    slot_list = jnp.arange(ep * id_slots, dtype=jnp.int32)
    local_id = next_ids - holder * vocab + 1
    asked = jnp.sum(jnp.where(slot_list[:, None] == place[None, :], local_id[None, :], 0), axis=1)
    asked = jnp.broadcast_to(asked.reshape(ep, id_slots, 1), (ep, id_slots, 128))
    listed = jnp.broadcast_to(place[None, None, :], (ep, id_slots, tokens))
    asked = jnp.concatenate([asked, listed], axis=1)
    ids = lax.all_to_all(asked, EP, split_axis=0, concat_axis=0, tiled=True)

    def moved(half, gate):
        own = after(proj_weight[half], gate)
        return {0: own, **{by: shift(own, "ep_0", by) for by in (1, 3, 2)}}

    def lined(pieces):
        whole = jnp.zeros((4, padded(proj_weight.shape[1]), width), BF)
        for by, piece in pieces.items():
            whole = lax.dynamic_update_slice(whole, piece[None], (t ^ ((y - by) % 4), 0, 0))
        return whole.reshape(-1, width)

    hidden_pieces = moved(0, asked)

    def of_pair(shard):
        other = shift(shard, "ep_2", 1)
        return jnp.where(
            z == 0, jnp.concatenate([shard, other]), jnp.concatenate([other, shard])
        )

    gate_up_row = of_pair(after(shared_gate_up, asked))
    gate_up_row = stacked(
        gate_up_row, "ep_1", {by: shift(gate_up_row, "ep_1", by) for by in (1, 3, 2)}
    ).reshape(-1, *shared_gate_up.shape[1:])
    down_row = of_pair(after(shared_down, asked))

    wide_hidden = after(hidden_in, asked).astype(F32)
    wide_table = after(embed_table, asked).astype(F32)
    squares = jnp.concatenate(
        [jnp.sum(wide_table * wide_table, axis=1), jnp.sum(wide_hidden * wide_hidden, axis=1)]
    ).reshape(-1, 128)
    squares = squares + swap(squares, 1)
    squares = (squares + swap(squares, 2)).reshape(-1)
    scales = lax.rsqrt(squares / model + 1e-06)
    hidden_gain = lax.dynamic_slice(hidden_gain, (t * width,), (width,))[None, :]
    embed_gain = lax.dynamic_slice(embed_gain, (t * width,), (width,))[None, :]

    def over_tp(own):
        other = swap(own, 2)
        return [own, swap(own, 1), other, swap(other, 1)]

    blocks = feature_blocks(hidden_in, scales[vocab:, None], hidden_gain, plane)
    blocks = lax.all_to_all(blocks, XZ, split_axis=0, concat_axis=0, tiled=True)

    def side_by_side(own):
        return jnp.concatenate(over_tp(own.reshape(plane * tokens, -1)), axis=1)

    hidden_acts = side_by_side(blocks)

    found = found_blocks(ids, embed_table, scales[None, :vocab], embed_gain, planes, plane)
    found = after(found.reshape(ep, plane * id_slots, -1), blocks)
    embed_pieces = moved(1, found)
    gain_column = ffn_gain[:, None]

    def columns(which, gate):
        return gained_columns(
            jnp.stack(which).astype(jnp.int32), after(w_gate_up, gate), gain_column, 4
        )

    far_columns = columns([t ^ 3, t ^ 1], found)
    found = lax.all_to_all(found, EP, split_axis=0, concat_axis=0, tiled=True)
    first = (y * plane).astype(jnp.int32).reshape(1)
    found, far_columns = together(found, far_columns)
    embed_blocks = picked_blocks(first, found, ids, plane, tokens)
    for by in (1, 3, 2):
        hidden_pieces[by] = after(hidden_pieces[by], embed_blocks)
    hidden_acts = after(hidden_acts, embed_blocks)
    start = product(hidden_acts, lined(hidden_pieces)).astype(BF)
    embed_acts = side_by_side(embed_blocks)
    for by in (1, 3, 2):
        embed_pieces[by] = after(embed_pieces[by], start)
    embed_acts, gate_up_row, down_row, start = together(embed_acts, gate_up_row, down_row, start)
    partial = (product(embed_acts, lined(embed_pieces)) + start.astype(F32)).astype(BF)

    top = routes.shape[1]
    capacity = min(tokens, tokens * top * 5 // (4 * ep))
    routes = after(routes, partial)
    named = routes[:, :, None] == experts[None, None, :]
    hits = jnp.any(named, axis=1)
    share = jnp.sum(jnp.where(named, route_weights[:, :, None], 0.0), axis=1)
    rank = jnp.where(hits, ranked(hits), -1)
    taken = rank.T[:, None, :] == jnp.arange(capacity, dtype=jnp.int32)[None, :, None]
    send = taken.astype(BF).reshape(ep * capacity, tokens)
    combine = jnp.where(taken, share.T[:, None, :], 0.0).astype(BF)
    combine = combine.reshape(ep * capacity, tokens)

    near_columns = columns([t ^ 2, t], partial)
    down_block = after(w_down, partial).reshape(4, -1, width)
    down_block = jnp.concatenate(
        [lax.dynamic_index_in_dim(down_block, t ^ q, 0, keepdims=False) for q in range(4)]
    )

    gate_up_row = after(gate_up_row, partial)
    gate_up_lines = {by: shift(gate_up_row, "ep_0", by) for by in (1, 3)}
    down_row = after(down_row, partial)
    down_row = stacked(down_row, "ep_0", {by: shift(down_row, "ep_0", by) for by in (1, 3, 2)})
    sums = lax.all_to_all(
        partial.reshape(plane, tokens, width), XZ, split_axis=0, concat_axis=0, tiled=True
    )
    sums, near_columns, down_block, send, combine, gate_up_lines[1], gate_up_lines[3] = together(
        sums, near_columns, down_block, send, combine, gate_up_lines[1], gate_up_lines[3]
    )
    projected = sums.astype(F32).sum(axis=0).astype(BF)

    outgoing = jnp.dot(send, projected, preferred_element_type=F32).astype(BF)
    arrived = lax.all_to_all(
        outgoing.reshape(ep, capacity, width), EP, split_axis=0, concat_axis=0, tiled=True
    )
    wide = projected.astype(F32)
    squares = jnp.sum(wide * wide, axis=1).reshape(1, tokens)
    squares = squares + swap(squares, 1)
    squares = squares + swap(squares, 2)
    row_scale = lax.rsqrt(squares / model + 1e-06).reshape(tokens, 1)

    def gated(pair, scale):
        hidden = pair.shape[-1] // 2
        pair = pair * scale
        return (jax.nn.silu(pair[:, :hidden]) * pair[:, hidden:]).astype(BF)

    rows = arrived.reshape(ep * capacity, width)
    far = swap(product(rows, far_columns).astype(BF), 1)
    near = product(rows, near_columns).astype(BF)
    half = near.shape[1] // 2

    def both(a, b, part):
        return a[:, part * half :][:, :half].astype(F32) + b[:, part * half :][:, :half].astype(F32)

    across = both(far, near, 0).astype(BF)
    wide = after(rows, across).astype(F32)
    squares = jnp.sum(wide * wide, axis=1).reshape(-1, 128)
    squares = squares + swap(squares, 1)
    squares = squares + swap(squares, 2)
    slot_scale = lax.rsqrt(squares / model + 1e-06).reshape(-1, 1)
    gate_up_lines[2] = shift(after(gate_up_row, arrived), "ep_0", 2)
    down_row = after(down_row, arrived)
    down_lines = {by: shift(down_row, "ep_1", by) for by in (1, 3, 2)}
    across = swap(across, 2)
    across, gate_up_lines[2], down_lines[1], down_lines[2], down_lines[3] = together(
        across, gate_up_lines[2], down_lines[1], down_lines[2], down_lines[3]
    )
    act = gated(both(far, near, 1) + across.astype(F32), slot_scale)
    acts = jnp.concatenate(over_tp(act), axis=1)
    result = product(acts, down_block).astype(BF)
    returned = lax.all_to_all(
        result.reshape(ep, capacity, width), EP, split_axis=0, concat_axis=0, tiled=True
    )

    gate_up_row, down_row = after(gate_up_row, result), after(down_row, result)
    shared_columns = stacked(gate_up_row, "ep_0", gate_up_lines).reshape(width, 2, -1)
    shared_columns = jnp.concatenate(
        [(shared_columns[:, j].astype(F32) * gain_column).astype(BF) for j in range(2)], axis=1
    )
    shared_pair = product(projected, shared_columns).astype(BF).reshape(tokens, 2, 4, -1)

    def of_tp(which):
        block = lax.dynamic_index_in_dim(shared_pair, which, 2, keepdims=False)
        return block.reshape(tokens, -1).astype(F32)

    def sent(which):
        return of_tp(which).astype(BF)

    far = [swap(sent(t ^ 3), 1), swap(sent(t ^ 1), 1)]
    across = swap((far[0].astype(F32) + of_tp(t ^ 2)).astype(BF), 2)
    act = gated(far[1].astype(F32) + of_tp(t) + across.astype(F32), row_scale)
    shared_acts = jnp.stack(over_tp(act))
    shared_acts = jnp.concatenate(
        [lax.dynamic_index_in_dim(shared_acts, t ^ q, 0, keepdims=False) for q in range(4)], axis=1
    )
    shared_rows = jnp.zeros((4, 4, down_row.shape[1], width), BF)
    for by, piece in {0: down_row, **down_lines}.items():
        shared_rows = lax.dynamic_update_slice(
            shared_rows, piece[:, None], (0, (x - by) % 4, 0, 0)
        )
    shared = product(shared_acts, shared_rows.reshape(-1, width))

    returned, shared = together(returned, shared)
    routed = lax.dot_general(
        combine,
        returned.reshape(ep * capacity, width),
        (((0,), (0,)), ((), ())),
        preferred_element_type=F32,
    )
    return (projected.astype(F32) + routed + shared).astype(BF)


def solution(mesh):
    finer = Mesh(mesh.devices.reshape(mesh.shape["tp"], 4, 4, 2), ("tp", "ep_0", "ep_1", "ep_2"))
    in_specs = (
        P(EP, "tp"),
        P(EP),
        P(EP, "tp"),
        P(),
        P(),
        P("tp"),
        P(None, EP, "tp"),
        P(EP, None),
        P(EP, None),
        P(EP, "tp", None, None),
        P(EP, None, "tp"),
        P(TP_EP, None, None),
        P(EP, "tp"),
    )
    out_specs = P(EP, "tp")

    def body(*args):
        args = list(args)
        args[9] = args[9].reshape(args[9].shape[1:])
        return on_device(*args)

    return jax.shard_map(body, mesh=finer, in_specs=in_specs, out_specs=out_specs, check_vma=False)
```

```python
import jax
import jax.numpy as jnp
from jax import lax
from jax.experimental import pallas as pl
from jax.experimental.pallas import tpu as pltpu
from jax.sharding import Mesh
from jax.sharding import PartitionSpec as P

EP = ("ep_0", "ep_1", "ep_2")
XZ = ("ep_1", "ep_2")
TP_EP = ("tp", "ep_0", "ep_1", "ep_2")
BF = jnp.bfloat16
F32 = jnp.float32


def params(*semantics):
    return pltpu.CompilerParams(dimension_semantics=semantics)


def cost(flops, moved):
    return pl.CostEstimate(flops=int(flops), bytes_accessed=int(moved), transcendentals=0)


def swap(value, bit):
    return lax.ppermute(value, "tp", [(i, i ^ bit) for i in range(4)])


def shift(value, axis, by):
    size = lax.axis_size(axis)
    return lax.ppermute(value, axis, [(i, (i + by) % size) for i in range(size)])


def after(value, *earlier):
    return lax.optimization_barrier((value, *earlier))[0]


def together(*values):
    return lax.optimization_barrier(values)


def stacked(value, axis, moved):
    me = lax.axis_index(axis)
    whole = jnp.zeros((4, *value.shape), value.dtype)
    for by, piece in moved.items():
        whole = lax.dynamic_update_index_in_dim(whole, piece, (me - by) % 4, 0)
    return lax.dynamic_update_index_in_dim(whole, value, me, 0)


def padded(part):
    return -(-part // 128) * 128


def feature_blocks(rows, scale, gain, count):
    n, width = rows.shape
    part = width // count
    room = padded(part)

    def kernel(x_ref, s_ref, g_ref, o_ref):
        v = x_ref[...].astype(F32) * s_ref[...] * g_ref[...]
        o_ref[...] = jnp.zeros_like(o_ref)
        for b in range(count):
            o_ref[b, :, 0:part] = v[:, b * part : (b + 1) * part].astype(BF)

    return pl.pallas_call(
        kernel,
        out_shape=jax.ShapeDtypeStruct((count, n, room), BF),
        cost_estimate=cost(4 * n * width, 4 * n * width),
    )(rows, scale, gain)


def found_blocks(asked, table, scales, gain, planes, count):
    holders, half = asked.shape[0], asked.shape[1] // 2
    slots = holders * half
    vocab, width = table.shape
    part = width // count
    room = padded(part)
    step = 512
    each = slots // planes

    def kernel(i_ref, t_ref, s_ref, g_ref, o_ref, acc, sc):
        k = pl.program_id(0)

        @pl.when(k == 0)
        def _():
            acc[...] = jnp.zeros_like(acc)
            sc[...] = jnp.zeros_like(sc)

        ids = i_ref[...].reshape(slots, 128)[:, 0:1] - 1
        hit = ids == lax.broadcasted_iota(jnp.int32, (slots, step), 1) + k * step
        acc[...] += jnp.dot(
            jnp.where(hit, 1.0, 0.0).astype(BF), t_ref[...], preferred_element_type=F32
        )
        sc[...] += jnp.sum(jnp.where(hit, s_ref[...], 0.0), axis=1, keepdims=True)

        @pl.when(k == pl.num_programs(0) - 1)
        def _():
            v = acc[...] * sc[...] * g_ref[...]
            o_ref[...] = jnp.zeros_like(o_ref)
            for b in range(count):
                piece = v[:, b * part : (b + 1) * part].astype(BF)
                for y in range(planes):
                    o_ref[y, b, :, 0:part] = piece[y * each : (y + 1) * each]

    return pl.pallas_call(
        kernel,
        grid=(vocab // step,),
        in_specs=[
            pl.BlockSpec((holders, half, 128), lambda k: (0, 0, 0)),
            pl.BlockSpec((step, width), lambda k: (k, 0)),
            pl.BlockSpec((1, step), lambda k: (0, k)),
            pl.BlockSpec((1, width), lambda k: (0, 0)),
        ],
        out_specs=pl.BlockSpec((planes, count, each, room), lambda k: (0, 0, 0, 0)),
        out_shape=jax.ShapeDtypeStruct((planes, count, each, room), BF),
        scratch_shapes=[pltpu.VMEM((slots, width), F32), pltpu.VMEM((slots, 1), F32)],
        compiler_params=params("arbitrary"),
        cost_estimate=cost(2 * slots * vocab * width, 2 * vocab * width),
    )(asked, table, scales, gain)


def picked_blocks(first, arrived, asked, sources, tokens):
    holders, rows, room = arrived.shape
    each = rows // sources
    slots = holders * each

    def kernel(f_ref, a_ref, p_ref, o_ref):
        hit = lax.broadcasted_iota(jnp.int32, (slots, tokens), 0) == p_ref[0, 0:1, :]
        o_ref[0] = lax.dot_general(
            jnp.where(hit, 1.0, 0.0).astype(BF),
            a_ref[...].reshape(slots, room),
            (((0,), (0,)), ((), ())),
            preferred_element_type=F32,
        ).astype(BF)

    return pl.pallas_call(
        kernel,
        grid_spec=pltpu.PrefetchScalarGridSpec(
            num_scalar_prefetch=1,
            grid=(sources,),
            in_specs=[
                pl.BlockSpec((holders, each, room), lambda s, f: (0, s, 0)),
                pl.BlockSpec((1, asked.shape[1] // 2, tokens), lambda s, f: (f[0] + s, 1, 0)),
            ],
            out_specs=pl.BlockSpec((1, tokens, room), lambda s, f: (s, 0, 0)),
        ),
        out_shape=jax.ShapeDtypeStruct((sources, tokens, room), BF),
        compiler_params=params("arbitrary"),
        cost_estimate=cost(2 * sources * slots * tokens * room, 4 * holders * rows * room),
    )(first, arrived, asked)


def gained_columns(blocks, weights, gain, count):
    depth, _, width = weights.shape
    part = width // count
    step = depth // 8
    picked = blocks.shape[0]

    def kernel(at, w_ref, g_ref, o_ref):
        g = g_ref[...]
        o_ref[:, 0:part] = (w_ref[:, 0, :].astype(F32) * g).astype(BF)
        o_ref[:, part : 2 * part] = (w_ref[:, 1, :].astype(F32) * g).astype(BF)

    return pl.pallas_call(
        kernel,
        grid_spec=pltpu.PrefetchScalarGridSpec(
            num_scalar_prefetch=1,
            grid=(8, picked),
            in_specs=[
                pl.BlockSpec((step, 2, part), lambda k, b, at: (k, 0, at[b])),
                pl.BlockSpec((step, 1), lambda k, b, at: (k, 0)),
            ],
            out_specs=pl.BlockSpec((step, 2 * part), lambda k, b, at: (k, b)),
        ),
        out_shape=jax.ShapeDtypeStruct((depth, picked * 2 * part), BF),
        compiler_params=params("arbitrary", "arbitrary"),
        cost_estimate=cost(2 * depth * width, 4 * depth * width),
    )(blocks, weights, gain)


def product(rows, weights):
    return jnp.dot(rows, weights, preferred_element_type=F32)


def ranked(marks):
    rows = marks.shape[0]
    below = jnp.tril(jnp.ones((rows, rows), BF), -1)
    return jnp.dot(below, marks.astype(BF), preferred_element_type=F32).astype(jnp.int32)


def on_device(
    hidden_in,
    next_ids,
    embed_table,
    hidden_gain,
    embed_gain,
    ffn_gain,
    proj_weight,
    routes,
    route_weights,
    w_gate_up,
    w_down,
    shared_gate_up,
    shared_down,
):
    tokens, width = hidden_in.shape
    ep = lax.axis_size(EP)
    plane = lax.axis_size(XZ)
    planes = ep // plane
    vocab = embed_table.shape[0]
    model = width * 4
    t = lax.axis_index("tp")
    y = lax.axis_index("ep_0")
    x = lax.axis_index("ep_1")
    z = lax.axis_index("ep_2")
    experts = jnp.arange(ep, dtype=jnp.int32)

    id_slots = 2 * tokens // ep
    holder = next_ids // vocab
    marks = holder[:, None] == experts[None, :]
    order = jnp.sum(jnp.where(marks, ranked(marks), 0), axis=1)
    place = holder * id_slots + order
    slot_list = jnp.arange(ep * id_slots, dtype=jnp.int32)
    local_id = next_ids - holder * vocab + 1
    asked = jnp.sum(jnp.where(slot_list[:, None] == place[None, :], local_id[None, :], 0), axis=1)
    asked = jnp.broadcast_to(asked.reshape(ep, id_slots, 1), (ep, id_slots, 128))
    listed = jnp.broadcast_to(place[None, None, :], (ep, id_slots, tokens))
    asked = jnp.concatenate([asked, listed], axis=1)
    ids = lax.all_to_all(asked, EP, split_axis=0, concat_axis=0, tiled=True)

    def moved(half, gate, steps):
        own = after(proj_weight[half], gate)
        return {0: own, **{by: shift(own, "ep_0", by) for by in steps}}

    def lined(pieces):
        whole = jnp.zeros((4, padded(proj_weight.shape[1]), width), BF)
        for by, piece in pieces.items():
            whole = lax.dynamic_update_slice(whole, piece[None], (t ^ ((y - by) % 4), 0, 0))
        return whole.reshape(-1, width)

    hidden_pieces = moved(0, asked, (1, 3, 2))

    wide_hidden = after(hidden_in, asked).astype(F32)
    wide_table = after(embed_table, asked).astype(F32)
    squares = jnp.sum(wide_table * wide_table, axis=1)
    squares = jnp.concatenate([squares, jnp.sum(wide_hidden * wide_hidden, axis=1)])
    squares = squares.reshape(-1, 128)
    squares = squares + swap(squares, 1)
    squares = (squares + swap(squares, 2)).reshape(-1)
    scales = lax.rsqrt(squares / model + 1e-06)
    hidden_gain = lax.dynamic_slice(hidden_gain, (t * width,), (width,))[None, :]
    embed_gain = lax.dynamic_slice(embed_gain, (t * width,), (width,))[None, :]

    def over_tp(own):
        other = swap(own, 2)
        return [own, swap(own, 1), other, swap(other, 1)]

    blocks = feature_blocks(hidden_in, scales[vocab:, None], hidden_gain, plane)
    blocks = lax.all_to_all(blocks, XZ, split_axis=0, concat_axis=0, tiled=True)

    def side_by_side(own):
        return jnp.concatenate(over_tp(own.reshape(plane * tokens, -1)), axis=1)

    found = found_blocks(ids, embed_table, scales[None, :vocab], embed_gain, planes, plane)
    found = after(found.reshape(ep, plane * id_slots, -1), blocks)
    embed_pieces = moved(1, found, (1, 3, 2))
    gain_column = ffn_gain[:, None]

    def columns(which, gate):
        return gained_columns(
            jnp.stack(which).astype(jnp.int32), after(w_gate_up, gate), gain_column, 4
        )

    def both_of_pair(shard):
        return shard, shift(shard, "ep_2", 1)

    def of_pair(own, other, gate):
        other = after(other, gate)
        return jnp.where(z == 0, jnp.concatenate([own, other]), jnp.concatenate([other, own]))

    def of_line(row, axis):
        return stacked(row, axis, {by: shift(row, axis, by) for by in (1, 3, 2)})

    gate_up_row = both_of_pair(after(shared_gate_up, found))
    down_row = both_of_pair(after(shared_down, found))

    found = lax.all_to_all(found, EP, split_axis=0, concat_axis=0, tiled=True)
    first = (y * plane).astype(jnp.int32).reshape(1)
    embed_blocks = picked_blocks(first, found, ids, plane, tokens)
    embed_acts = side_by_side(embed_blocks)
    hidden_acts = side_by_side(blocks)
    for by in (1, 3, 2):
        hidden_pieces[by] = after(hidden_pieces[by], embed_blocks)
    start = product(hidden_acts, lined(hidden_pieces)).astype(BF)
    gate_up_row = of_pair(*gate_up_row, embed_blocks)
    down_row = of_pair(*down_row, embed_blocks)
    gate_up_row = of_line(gate_up_row, "ep_1")
    gate_up_row = gate_up_row.reshape(-1, *shared_gate_up.shape[1:])
    for by in (1, 3, 2):
        embed_pieces[by] = after(embed_pieces[by], start)
    partial = (product(embed_acts, lined(embed_pieces)) + start.astype(F32)).astype(BF)

    top = routes.shape[1]
    capacity = min(tokens, tokens * top * 5 // (4 * ep))
    routes = after(routes, partial)
    named = routes[:, :, None] == experts[None, None, :]
    hits = jnp.any(named, axis=1)
    share = jnp.sum(jnp.where(named, route_weights[:, :, None], 0.0), axis=1)
    rank = jnp.where(hits, ranked(hits), -1)
    taken = rank.T[:, None, :] == jnp.arange(capacity, dtype=jnp.int32)[None, :, None]
    send = taken.astype(BF).reshape(ep * capacity, tokens)
    combine = jnp.where(taken, share.T[:, None, :], 0.0).astype(BF)
    combine = combine.reshape(ep * capacity, tokens)

    far_columns = columns([t ^ 3, t ^ 1], partial)
    near_columns = columns([t ^ 2, t], partial)
    down_block = after(w_down, partial).reshape(4, -1, width)
    down_block = jnp.concatenate(
        [lax.dynamic_index_in_dim(down_block, t ^ q, 0, keepdims=False) for q in range(4)]
    )

    gate_up_row = after(gate_up_row, partial)
    gate_up_lines = {by: shift(gate_up_row, "ep_0", by) for by in (1, 3)}
    down_row = of_line(after(down_row, partial), "ep_0")
    sums = lax.all_to_all(
        partial.reshape(plane, tokens, width), XZ, split_axis=0, concat_axis=0, tiled=True
    )
    sums, far_columns, near_columns, down_block, send, combine = together(
        sums, far_columns, near_columns, down_block, send, combine
    )
    sums, down_row, gate_up_lines[1], gate_up_lines[3] = together(
        sums, down_row, gate_up_lines[1], gate_up_lines[3]
    )
    projected = sums.astype(F32).sum(axis=0).astype(BF)

    outgoing = jnp.dot(send, projected, preferred_element_type=F32).astype(BF)
    arrived = lax.all_to_all(
        outgoing.reshape(ep, capacity, width), EP, split_axis=0, concat_axis=0, tiled=True
    )

    def gated(pair, scale):
        hidden = pair.shape[-1] // 2
        pair = pair * scale
        return (jax.nn.silu(pair[:, :hidden]) * pair[:, hidden:]).astype(BF)

    rows = arrived.reshape(ep * capacity, width)
    gate_up_lines[2] = shift(after(gate_up_row, arrived), "ep_0", 2)
    down_row = after(down_row, arrived)
    down_lines = {by: shift(down_row, "ep_1", by) for by in (1, 3, 2)}
    far = product(rows, far_columns).astype(BF)
    far = swap(far, 1)
    near = product(rows, near_columns).astype(BF)
    half = near.shape[1] // 2

    def both(a, b, part):
        return a[:, part * half :][:, :half].astype(F32) + b[:, part * half :][:, :half].astype(F32)

    across = both(far, near, 0).astype(BF)
    wide = after(rows, across).astype(F32)
    squares = jnp.sum(wide * wide, axis=1).reshape(-1, 128)
    squares = squares + swap(squares, 1)
    squares = squares + swap(squares, 2)
    slot_scale = lax.rsqrt(squares / model + 1e-06).reshape(-1, 1)
    across = swap(across, 2)
    act = gated(both(far, near, 1) + across.astype(F32), slot_scale)
    acts = jnp.concatenate(over_tp(act), axis=1)
    acts, gate_up_lines[2] = together(acts, gate_up_lines[2])
    for by in (1, 3, 2):
        acts, down_lines[by] = together(acts, down_lines[by])
    result = product(acts, down_block).astype(BF)
    returned = lax.all_to_all(
        result.reshape(ep, capacity, width), EP, split_axis=0, concat_axis=0, tiled=True
    )

    wide = after(projected, result).astype(F32)
    squares = jnp.sum(wide * wide, axis=1).reshape(1, tokens)
    squares = squares + swap(squares, 1)
    squares = squares + swap(squares, 2)
    row_scale = lax.rsqrt(squares / model + 1e-06).reshape(tokens, 1)

    gate_up_row, down_row = after(gate_up_row, result), after(down_row, result)
    shared_columns = stacked(gate_up_row, "ep_0", gate_up_lines).reshape(width, 2, -1)
    shared_columns = jnp.concatenate(
        [(shared_columns[:, j].astype(F32) * gain_column).astype(BF) for j in range(2)], axis=1
    )
    shared_pair = product(projected, shared_columns).astype(BF).reshape(tokens, 2, 4, -1)

    def of_tp(which):
        block = lax.dynamic_index_in_dim(shared_pair, which, 2, keepdims=False)
        return block.reshape(tokens, -1).astype(F32)

    def sent(which):
        return of_tp(which).astype(BF)

    far = [swap(sent(t ^ 3), 1), swap(sent(t ^ 1), 1)]
    across = swap((far[0].astype(F32) + of_tp(t ^ 2)).astype(BF), 2)
    act = gated(far[1].astype(F32) + of_tp(t) + across.astype(F32), row_scale)
    shared_acts = jnp.stack(over_tp(act))
    shared_acts = jnp.concatenate(
        [lax.dynamic_index_in_dim(shared_acts, t ^ q, 0, keepdims=False) for q in range(4)], axis=1
    )
    shared_rows = jnp.zeros((4, 4, down_row.shape[1], width), BF)
    for by, piece in {0: down_row, **down_lines}.items():
        shared_rows = lax.dynamic_update_slice(
            shared_rows, piece[:, None], (0, (x - by) % 4, 0, 0)
        )
    shared = product(shared_acts, shared_rows.reshape(-1, width))

    returned, shared = together(returned, shared)
    routed = lax.dot_general(
        combine,
        returned.reshape(ep * capacity, width),
        (((0,), (0,)), ((), ())),
        preferred_element_type=F32,
    )
    return (projected.astype(F32) + routed + shared).astype(BF)


def solution(mesh):
    finer = Mesh(mesh.devices.reshape(mesh.shape["tp"], 4, 4, 2), ("tp", "ep_0", "ep_1", "ep_2"))
    in_specs = (
        P(EP, "tp"),
        P(EP),
        P(EP, "tp"),
        P(),
        P(),
        P("tp"),
        P(None, EP, "tp"),
        P(EP, None),
        P(EP, None),
        P(EP, "tp", None, None),
        P(EP, None, "tp"),
        P(TP_EP, None, None),
        P(EP, "tp"),
    )
    out_specs = P(EP, "tp")

    def body(*args):
        args = list(args)
        args[9] = args[9].reshape(args[9].shape[1:])
        return on_device(*args)

    return jax.shard_map(body, mesh=finer, in_specs=in_specs, out_specs=out_specs, check_vma=False)
```

```python
import jax
import jax.numpy as jnp
from jax import lax
from jax.experimental import pallas as pl
from jax.experimental.pallas import tpu as pltpu
from jax.sharding import Mesh
from jax.sharding import PartitionSpec as P

EP = ("ep_0", "ep_1", "ep_2")
XZ = ("ep_1", "ep_2")
TP_EP = ("tp", "ep_0", "ep_1", "ep_2")
BF = jnp.bfloat16
F32 = jnp.float32


def params(*semantics):
    return pltpu.CompilerParams(dimension_semantics=semantics)


def cost(flops, moved):
    return pl.CostEstimate(flops=int(flops), bytes_accessed=int(moved), transcendentals=0)


def swap(value, bit):
    return lax.ppermute(value, "tp", [(i, i ^ bit) for i in range(4)])


def shift(value, axis, by):
    size = lax.axis_size(axis)
    return lax.ppermute(value, axis, [(i, (i + by) % size) for i in range(size)])


def after(value, *earlier):
    return lax.optimization_barrier((value, *earlier))[0]


def together(*values):
    return lax.optimization_barrier(values)


def stacked(value, axis, moved):
    me = lax.axis_index(axis)
    whole = jnp.zeros((4, *value.shape), value.dtype)
    for by, piece in moved.items():
        whole = lax.dynamic_update_index_in_dim(whole, piece, (me - by) % 4, 0)
    return lax.dynamic_update_index_in_dim(whole, value, me, 0)


def padded(part):
    return -(-part // 128) * 128


def feature_blocks(rows, scale, gain, count):
    n, width = rows.shape
    part = width // count
    room = padded(part)

    def kernel(x_ref, s_ref, g_ref, o_ref):
        v = x_ref[...].astype(F32) * s_ref[...] * g_ref[...]
        o_ref[...] = jnp.zeros_like(o_ref)
        for b in range(count):
            o_ref[b, :, 0:part] = v[:, b * part : (b + 1) * part].astype(BF)

    return pl.pallas_call(
        kernel,
        out_shape=jax.ShapeDtypeStruct((count, n, room), BF),
        cost_estimate=cost(4 * n * width, 4 * n * width),
    )(rows, scale, gain)


def found_blocks(asked, table, scales, gain, planes, count):
    holders, half = asked.shape[0], asked.shape[1] // 2
    slots = holders * half
    vocab, width = table.shape
    part = width // count
    room = padded(part)
    step = 512
    each = slots // planes

    def kernel(i_ref, t_ref, s_ref, g_ref, o_ref, acc, sc):
        k = pl.program_id(0)

        @pl.when(k == 0)
        def _():
            acc[...] = jnp.zeros_like(acc)
            sc[...] = jnp.zeros_like(sc)

        ids = i_ref[...].reshape(slots, 128)[:, 0:1] - 1
        hit = ids == lax.broadcasted_iota(jnp.int32, (slots, step), 1) + k * step
        acc[...] += jnp.dot(
            jnp.where(hit, 1.0, 0.0).astype(BF), t_ref[...], preferred_element_type=F32
        )
        sc[...] += jnp.sum(jnp.where(hit, s_ref[...], 0.0), axis=1, keepdims=True)

        @pl.when(k == pl.num_programs(0) - 1)
        def _():
            v = acc[...] * sc[...] * g_ref[...]
            o_ref[...] = jnp.zeros_like(o_ref)
            for b in range(count):
                piece = v[:, b * part : (b + 1) * part].astype(BF)
                for y in range(planes):
                    o_ref[y, b, :, 0:part] = piece[y * each : (y + 1) * each]

    return pl.pallas_call(
        kernel,
        grid=(vocab // step,),
        in_specs=[
            pl.BlockSpec((holders, half, 128), lambda k: (0, 0, 0)),
            pl.BlockSpec((step, width), lambda k: (k, 0)),
            pl.BlockSpec((1, step), lambda k: (0, k)),
            pl.BlockSpec((1, width), lambda k: (0, 0)),
        ],
        out_specs=pl.BlockSpec((planes, count, each, room), lambda k: (0, 0, 0, 0)),
        out_shape=jax.ShapeDtypeStruct((planes, count, each, room), BF),
        scratch_shapes=[pltpu.VMEM((slots, width), F32), pltpu.VMEM((slots, 1), F32)],
        compiler_params=params("arbitrary"),
        cost_estimate=cost(2 * slots * vocab * width, 2 * vocab * width),
    )(asked, table, scales, gain)


def picked_blocks(first, arrived, asked, sources, tokens):
    holders, rows, room = arrived.shape
    each = rows // sources
    slots = holders * each

    def kernel(f_ref, a_ref, p_ref, o_ref):
        hit = lax.broadcasted_iota(jnp.int32, (slots, tokens), 0) == p_ref[0, 0:1, :]
        o_ref[0] = lax.dot_general(
            jnp.where(hit, 1.0, 0.0).astype(BF),
            a_ref[...].reshape(slots, room),
            (((0,), (0,)), ((), ())),
            preferred_element_type=F32,
        ).astype(BF)

    return pl.pallas_call(
        kernel,
        grid_spec=pltpu.PrefetchScalarGridSpec(
            num_scalar_prefetch=1,
            grid=(sources,),
            in_specs=[
                pl.BlockSpec((holders, each, room), lambda s, f: (0, s, 0)),
                pl.BlockSpec((1, asked.shape[1] // 2, tokens), lambda s, f: (f[0] + s, 1, 0)),
            ],
            out_specs=pl.BlockSpec((1, tokens, room), lambda s, f: (s, 0, 0)),
        ),
        out_shape=jax.ShapeDtypeStruct((sources, tokens, room), BF),
        compiler_params=params("arbitrary"),
        cost_estimate=cost(2 * sources * slots * tokens * room, 4 * holders * rows * room),
    )(first, arrived, asked)


def gained_columns(blocks, weights, gain, count):
    depth, _, width = weights.shape
    part = width // count
    step = depth // 8
    picked = blocks.shape[0]

    def kernel(at, w_ref, g_ref, o_ref):
        g = g_ref[...]
        o_ref[:, 0:part] = (w_ref[:, 0, :].astype(F32) * g).astype(BF)
        o_ref[:, part : 2 * part] = (w_ref[:, 1, :].astype(F32) * g).astype(BF)

    return pl.pallas_call(
        kernel,
        grid_spec=pltpu.PrefetchScalarGridSpec(
            num_scalar_prefetch=1,
            grid=(8, picked),
            in_specs=[
                pl.BlockSpec((step, 2, part), lambda k, b, at: (k, 0, at[b])),
                pl.BlockSpec((step, 1), lambda k, b, at: (k, 0)),
            ],
            out_specs=pl.BlockSpec((step, 2 * part), lambda k, b, at: (k, b)),
        ),
        out_shape=jax.ShapeDtypeStruct((depth, picked * 2 * part), BF),
        compiler_params=params("arbitrary", "arbitrary"),
        cost_estimate=cost(2 * depth * width, 4 * depth * width),
    )(blocks, weights, gain)


def product(rows, weights):
    return jnp.dot(rows, weights, preferred_element_type=F32)


def ranked(marks):
    rows = marks.shape[0]
    below = jnp.tril(jnp.ones((rows, rows), BF), -1)
    return jnp.dot(below, marks.astype(BF), preferred_element_type=F32).astype(jnp.int32)


def on_device(
    hidden_in,
    next_ids,
    embed_table,
    hidden_gain,
    embed_gain,
    ffn_gain,
    proj_weight,
    routes,
    route_weights,
    w_gate_up,
    w_down,
    shared_gate_up,
    shared_down,
):
    tokens, width = hidden_in.shape
    ep = lax.axis_size(EP)
    plane = lax.axis_size(XZ)
    planes = ep // plane
    vocab = embed_table.shape[0]
    model = width * 4
    t = lax.axis_index("tp")
    y = lax.axis_index("ep_0")
    z = lax.axis_index("ep_2")
    experts = jnp.arange(ep, dtype=jnp.int32)

    id_slots = 2 * tokens // ep
    holder = next_ids // vocab
    marks = holder[:, None] == experts[None, :]
    order = jnp.sum(jnp.where(marks, ranked(marks), 0), axis=1)
    place = holder * id_slots + order
    slot_list = jnp.arange(ep * id_slots, dtype=jnp.int32)
    local_id = next_ids - holder * vocab + 1
    asked = jnp.sum(jnp.where(slot_list[:, None] == place[None, :], local_id[None, :], 0), axis=1)
    asked = jnp.broadcast_to(asked.reshape(ep, id_slots, 1), (ep, id_slots, 128))
    listed = jnp.broadcast_to(place[None, None, :], (ep, id_slots, tokens))
    asked = jnp.concatenate([asked, listed], axis=1)
    ids = lax.all_to_all(asked, EP, split_axis=0, concat_axis=0, tiled=True)

    def moved(half, gate, steps):
        own = after(proj_weight[half], gate)
        return {0: own, **{by: shift(own, "ep_0", by) for by in steps}}

    def lined(pieces):
        whole = jnp.zeros((4, padded(proj_weight.shape[1]), width), BF)
        for by, piece in pieces.items():
            whole = lax.dynamic_update_slice(whole, piece[None], (t ^ ((y - by) % 4), 0, 0))
        return whole.reshape(-1, width)

    hidden_pieces = moved(0, asked, (1, 3))

    wide_hidden = after(hidden_in, asked).astype(F32)
    wide_table = after(embed_table, asked).astype(F32)
    squares = jnp.sum(wide_table * wide_table, axis=1)
    squares = jnp.concatenate([squares, jnp.sum(wide_hidden * wide_hidden, axis=1)])
    squares = squares.reshape(-1, 128)
    squares = squares + swap(squares, 1)
    squares = (squares + swap(squares, 2)).reshape(-1)
    scales = lax.rsqrt(squares / model + 1e-06)
    hidden_gain = lax.dynamic_slice(hidden_gain, (t * width,), (width,))[None, :]
    embed_gain = lax.dynamic_slice(embed_gain, (t * width,), (width,))[None, :]

    def over_tp(own):
        other = swap(own, 2)
        return [own, swap(own, 1), other, swap(other, 1)]

    blocks = feature_blocks(hidden_in, scales[vocab:, None], hidden_gain, plane)
    blocks = lax.all_to_all(blocks, XZ, split_axis=0, concat_axis=0, tiled=True)

    def side_by_side(own):
        return jnp.concatenate(over_tp(own.reshape(plane * tokens, -1)), axis=1)

    found = found_blocks(ids, embed_table, scales[None, :vocab], embed_gain, planes, plane)
    found = after(found.reshape(ep, plane * id_slots, -1), blocks)
    hidden_pieces[2] = shift(after(hidden_pieces[1], found), "ep_0", 1)
    embed_pieces = moved(1, found, (1, 3))
    gain_column = ffn_gain[:, None]

    def columns(which, gate):
        return gained_columns(
            jnp.stack(which).astype(jnp.int32), after(w_gate_up, gate), gain_column, 4
        )

    def both_of_pair(shard):
        return shard, shift(shard, "ep_2", 1)

    def of_pair(own, other, gate):
        other = after(other, gate)
        return jnp.where(z == 0, jnp.concatenate([own, other]), jnp.concatenate([other, own]))

    def of_line(row, axis):
        return stacked(row, axis, {by: shift(row, axis, by) for by in (1, 3, 2)})

    gate_up_row = both_of_pair(after(shared_gate_up, found))
    down_row = both_of_pair(after(shared_down, found))

    found = lax.all_to_all(found, EP, split_axis=0, concat_axis=0, tiled=True)
    first = (y * plane).astype(jnp.int32).reshape(1)
    embed_blocks = picked_blocks(first, found, ids, plane, tokens)
    embed_acts = side_by_side(embed_blocks)
    embed_pieces[2] = shift(after(embed_pieces[3], embed_blocks), "ep_0", 3)
    hidden_acts = side_by_side(blocks)
    for by in (1, 3, 2):
        hidden_pieces[by] = after(hidden_pieces[by], embed_blocks)
    start = product(hidden_acts, lined(hidden_pieces)).astype(BF)
    gate_up_row = of_pair(*gate_up_row, embed_blocks)
    down_row = of_pair(*down_row, embed_blocks)
    gate_up_row = of_line(gate_up_row, "ep_1")
    down_row = of_line(down_row, "ep_1")
    gate_up_row = gate_up_row.reshape(-1, *shared_gate_up.shape[1:])
    for by in (1, 3, 2):
        embed_pieces[by] = after(embed_pieces[by], start)
    partial = (product(embed_acts, lined(embed_pieces)) + start.astype(F32)).astype(BF)

    top = routes.shape[1]
    capacity = min(tokens, tokens * top * 5 // (4 * ep))
    routes = after(routes, partial)
    named = routes[:, :, None] == experts[None, None, :]
    hits = jnp.any(named, axis=1)
    share = jnp.sum(jnp.where(named, route_weights[:, :, None], 0.0), axis=1)
    rank = jnp.where(hits, ranked(hits), -1)
    taken = rank.T[:, None, :] == jnp.arange(capacity, dtype=jnp.int32)[None, :, None]
    send = taken.astype(BF).reshape(ep * capacity, tokens)
    combine = jnp.where(taken, share.T[:, None, :], 0.0).astype(BF)
    combine = combine.reshape(ep * capacity, tokens)

    far_columns = columns([t ^ 3, t ^ 1], partial)
    near_columns = columns([t ^ 2, t], partial)
    down_block = after(w_down, partial).reshape(4, -1, width)
    down_block = jnp.concatenate(
        [lax.dynamic_index_in_dim(down_block, t ^ q, 0, keepdims=False) for q in range(4)]
    )

    gate_up_row, down_row, _ = together(gate_up_row, down_row, partial)
    gate_up_lines = {by: shift(gate_up_row, "ep_0", by) for by in (1, 3)}
    sums = lax.all_to_all(
        partial.reshape(plane, tokens, width), XZ, split_axis=0, concat_axis=0, tiled=True
    )
    sums, far_columns, near_columns, down_block, send, combine = together(
        sums, far_columns, near_columns, down_block, send, combine
    )
    sums, gate_up_lines[1], gate_up_lines[3] = together(
        sums, gate_up_lines[1], gate_up_lines[3]
    )
    projected = sums.astype(F32).sum(axis=0).astype(BF)

    outgoing = jnp.dot(send, projected, preferred_element_type=F32).astype(BF)
    arrived = lax.all_to_all(
        outgoing.reshape(ep, capacity, width), EP, split_axis=0, concat_axis=0, tiled=True
    )

    def gated(pair, scale):
        hidden = pair.shape[-1] // 2
        pair = pair * scale
        return (jax.nn.silu(pair[:, :hidden]) * pair[:, hidden:]).astype(BF)

    rows = arrived.reshape(ep * capacity, width)
    gate_up_lines[2] = shift(after(gate_up_row, arrived), "ep_0", 2)
    down_row = after(down_row, arrived)
    down_lines = {by: shift(down_row, "ep_0", by) for by in (1, 3, 2)}
    far = product(rows, far_columns).astype(BF)
    far = swap(far, 1)
    near = product(rows, near_columns).astype(BF)
    half = near.shape[1] // 2

    def both(a, b, part):
        return a[:, part * half :][:, :half].astype(F32) + b[:, part * half :][:, :half].astype(F32)

    across = both(far, near, 0).astype(BF)
    wide = after(rows, across).astype(F32)
    squares = jnp.sum(wide * wide, axis=1).reshape(-1, 128)
    squares = squares + swap(squares, 1)
    squares = squares + swap(squares, 2)
    slot_scale = lax.rsqrt(squares / model + 1e-06).reshape(-1, 1)
    across = swap(across, 2)
    act = gated(both(far, near, 1) + across.astype(F32), slot_scale)
    acts = jnp.concatenate(over_tp(act), axis=1)
    result = product(acts, down_block).astype(BF)
    returned = lax.all_to_all(
        result.reshape(ep, capacity, width), EP, split_axis=0, concat_axis=0, tiled=True
    )

    wide = after(projected, result).astype(F32)
    squares = jnp.sum(wide * wide, axis=1).reshape(1, tokens)
    squares = squares + swap(squares, 1)
    squares = squares + swap(squares, 2)
    row_scale = lax.rsqrt(squares / model + 1e-06).reshape(tokens, 1)

    gate_up_row, down_row = after(gate_up_row, result), after(down_row, result)
    for lines in (gate_up_lines, down_lines):
        for by in list(lines):
            lines[by] = after(lines[by], result)
    shared_columns = stacked(gate_up_row, "ep_0", gate_up_lines).reshape(width, 2, -1)
    shared_columns = jnp.concatenate(
        [(shared_columns[:, j].astype(F32) * gain_column).astype(BF) for j in range(2)], axis=1
    )
    shared_pair = product(projected, shared_columns).astype(BF).reshape(tokens, 2, 4, -1)

    def of_tp(which):
        block = lax.dynamic_index_in_dim(shared_pair, which, 2, keepdims=False)
        return block.reshape(tokens, -1).astype(F32)

    def sent(which):
        return of_tp(which).astype(BF)

    far = [swap(sent(t ^ 3), 1), swap(sent(t ^ 1), 1)]
    across = swap((far[0].astype(F32) + of_tp(t ^ 2)).astype(BF), 2)
    act = gated(far[1].astype(F32) + of_tp(t) + across.astype(F32), row_scale)
    shared_acts = jnp.stack(over_tp(act))
    shared_acts = jnp.concatenate(
        [lax.dynamic_index_in_dim(shared_acts, t ^ q, 0, keepdims=False) for q in range(4)], axis=1
    )
    shared_rows = stacked(down_row, "ep_0", down_lines)
    shared = product(shared_acts, shared_rows.reshape(-1, width))

    returned, shared = together(returned, shared)
    routed = lax.dot_general(
        combine,
        returned.reshape(ep * capacity, width),
        (((0,), (0,)), ((), ())),
        preferred_element_type=F32,
    )
    return (projected.astype(F32) + routed + shared).astype(BF)


def solution(mesh):
    finer = Mesh(mesh.devices.reshape(mesh.shape["tp"], 4, 4, 2), ("tp", "ep_0", "ep_1", "ep_2"))
    in_specs = (
        P(EP, "tp"),
        P(EP),
        P(EP, "tp"),
        P(),
        P(),
        P("tp"),
        P(None, EP, "tp"),
        P(EP, None),
        P(EP, None),
        P(EP, "tp", None, None),
        P(EP, None, "tp"),
        P(TP_EP, None, None),
        P(EP, "tp"),
    )
    out_specs = P(EP, "tp")

    def body(*args):
        args = list(args)
        args[9] = args[9].reshape(args[9].shape[1:])
        return on_device(*args)

    return jax.shard_map(body, mesh=finer, in_specs=in_specs, out_specs=out_specs, check_vma=False)
```
